512 devices in a mesh: island: 8 (over x, core), dp: 2 (over y_lo), expert: 32 (over y_hi, z).
Axes of the slice: x: 4, y: 4 (y_hi: 2, y_lo: 2; y = y_hi * 2 + y_lo), z: 16, core: 2. Of those that a mesh axis runs over, the one named last changes fastest.
Arguments:
- theta: bfloat16 [8, 32, 384, 2048], P('island', 'expert', 'dp'), may hold values from -7.5 to 7.5
- first_moment: bfloat16 [8, 32, 384, 2048], P('island', 'expert', 'dp'), may hold values from -0.119628906 to 0.119628906
- second_moment: bfloat16 [8, 32, 384, 2048], P('island', 'expert', 'dp'), may hold values from 9.9658966e-05 to 0.0099487305
- anchor: float32 [32, 384, 2048], P('expert', 'dp', 'island'), may hold values from -4.5 to 4.5
- momentum: float32 [32, 384, 2048], P('expert', 'dp', 'island'), may hold values from -1.8 to 1.8
- cotangent: bfloat16 [65536, 2048], P(('island', 'dp', 'expert')), may hold values from -6 to 6
- weights: float32 [65536, 8], P(('island', 'dp', 'expert')), may hold values from 0.05 to 0.3
- expert_ids: int32 [65536, 8], P(('island', 'dp', 'expert')), may hold values from 0 to 127, as said below
- expert_counts: int32 [512, 16], P(('island', 'dp', 'expert')), may hold values from 1 to 16, as said below
- hidden_saved: bfloat16 [8, 2, 32, 512, 384], P('island', 'dp', 'expert'), may hold values from -6 to 6
Outputs:
- anchor_new: float32 [32, 384, 2048], P('expert', 'dp', 'island')
- momentum_new: float32 [32, 384, 2048], P('expert', 'dp', 'island')
- d_hidden: bfloat16 [8, 2, 32, 512, 384], P('island', 'dp', 'expert')
The draws below stay inside these ranges and needn't reach their ends.
Inputs may be any that keep to these rules, and one draw needn't show every extreme that they name: `expert_ids`: in each block of 128 rows a row's ids are distinct, every id below 16 is named by 1 to 16 pairs of the block, and those counts equal expert_counts of the block. expert_counts[b, e] is the number of pairs of block b naming expert e.
All inputs are finite; a program needn't handle non-finite values.
Results may differ from the reference program's by a relative error of at most 0.014.
Values may be sent and summed in bfloat16 or wider, within the bound.
A program may use at most 64 MiB of HBM per device.

```python
import math
import jax
import jax.numpy as jnp
from jax import lax

D = 2048
FF = 768
EXPERTS_ALL = 128
TOP = 8
TOK_DEV = 128
CAP = 16
EXPERTS = 16
UNITS = 32
FF_UNIT = 384
SLOTS = 512
TOKENS = 65536
N_ISLAND = 8
N_DP = 2
N_EXPERT = 32


def routing_tables(key):
    blocks = TOKENS // TOK_DEV
    keys = jax.random.split(key, 8)
    hotness = jax.random.randint(keys[0], (EXPERTS,), 0, 4)
    is_hot = hotness == 0
    cold_counts = 1 + jax.random.randint(keys[1], (blocks, EXPERTS), 0, max(CAP // 2, 1))
    hot_low = 3 * CAP // 4
    hot_counts = hot_low + jax.random.randint(keys[7], (blocks, EXPERTS), 0, CAP - hot_low + 1)
    counts = jnp.where(is_hot[None, :], hot_counts, cold_counts).astype(jnp.int32)
    full_expert = jax.random.randint(keys[2], (), 0, EXPERTS)
    second_expert = jax.random.randint(keys[3], (blocks,), 0, EXPERTS)
    expert_range = jnp.arange(EXPERTS, dtype=jnp.int32)
    forced = (expert_range[None, :] == full_expert) | (expert_range[None, :] == second_expert[:, None])
    counts = jnp.where(forced, CAP, counts).astype(jnp.int32)
    run_ends = jnp.cumsum(counts, axis=1)
    position = jnp.arange(TOK_DEV * TOP, dtype=jnp.int32)
    owner = jnp.sum((position[None, :, None] >= run_ends[:, None, :]).astype(jnp.int32), axis=2)
    inside = position[None, :] < run_ends[:, -1:]
    window_ids = jnp.where(inside, owner, -1).reshape(blocks, TOP, TOK_DEV).transpose(0, 2, 1)
    others = EXPERTS_ALL - EXPERTS
    scores = jax.random.randint(keys[4], (blocks, TOK_DEV, others), 0, 1 << 20) * others + jnp.arange(others, dtype=jnp.int32)
    picks = lax.top_k(scores, TOP)[1].astype(jnp.int32) + EXPERTS
    combined = jnp.where(window_ids >= 0, window_ids, picks)
    row_keys = jax.random.randint(keys[5], (blocks, TOK_DEV), 0, 1 << 20) * TOK_DEV + jnp.arange(TOK_DEV, dtype=jnp.int32)
    row_order = jnp.argsort(row_keys, axis=1, stable=True)
    combined = jnp.take_along_axis(combined, row_order[:, :, None], axis=1)
    column_keys = jax.random.randint(keys[6], (blocks, TOK_DEV, TOP), 0, 1 << 20) * TOP + jnp.arange(TOP, dtype=jnp.int32)
    column_order = jnp.argsort(column_keys, axis=2, stable=True)
    combined = jnp.take_along_axis(combined, column_order, axis=2)
    return (combined.reshape(blocks * TOK_DEV, TOP).astype(jnp.int32), counts)


def draw_expert_ids(key, part):
    return routing_tables(jax.random.fold_in(key, 11))[0]


def draw_expert_counts(key, part):
    return routing_tables(jax.random.fold_in(key, 11))[1]


def outer_state(key):
    keys = jax.random.split(jax.random.fold_in(key, 23), 5)
    field_shape = (UNITS, FF_UNIT, D)
    anchor = 0.7 * jnp.clip(jax.random.normal(keys[1], field_shape, jnp.float32), -6.0, 6.0)
    drift = 0.6 * jnp.clip(jax.random.normal(keys[4], (N_ISLAND,) + field_shape, jnp.float32), -4.0, 4.0)
    theta = (anchor[None] + drift).astype(jnp.bfloat16)
    return (theta, anchor)


def draw_theta(key, part):
    return outer_state(key)[0]


def draw_anchor(key, part):
    return outer_state(key)[1]


def level_of(stream_key, dims, pieces, smallest, largest):
    def one(axis_at, parts):
        steps = jax.random.uniform(jax.random.fold_in(jax.random.fold_in(stream_key, 6), axis_at), (parts,), jnp.float32, smallest / len(pieces), largest / len(pieces))
        return jnp.repeat(jnp.exp(steps), dims[axis_at] // parts).reshape((-1,) + (1,) * (len(dims) - axis_at - 1))

    level = one(*pieces[0])
    for cut in pieces[1:]:
        level = level * one(*cut)
    return level


def noise(rng, extent, spread, bound, pieces=(), kind=jnp.bfloat16):
    level = level_of(rng, extent, pieces, -0.22, 0.18) if pieces else 1.0
    values = jax.random.normal(rng, extent, jnp.float32) * spread * level
    return jnp.minimum(jnp.maximum(values, -bound), bound).astype(kind)


def setup_inputs(seed: int = 0) -> dict:
    streams_of = jax.random.split(jax.random.key(seed), 11)
    return {
        "theta": draw_theta(jax.random.fold_in(streams_of[10], 71), 0),
        "first_moment": noise(streams_of[1], (N_ISLAND, UNITS, FF_UNIT, D), 0.02, 0.119628906, ((0, 8), (1, 32), (2, 2))),
        "second_moment": jnp.clip(jnp.exp(math.log(0.0099487305) - 4.603446 * jax.random.uniform(streams_of[2], (N_ISLAND, UNITS, FF_UNIT, D), jnp.float32) ** level_of(streams_of[2], (N_ISLAND, UNITS, FF_UNIT, D), ((0, 8), (1, 32), (2, 2)), -0.2, 0.2)), 9.965896606445312e-05, 0.0099487305).astype(jnp.bfloat16),
        "anchor": draw_anchor(jax.random.fold_in(streams_of[10], 71), 0),
        "momentum": noise(streams_of[4], (UNITS, FF_UNIT, D), 0.3, 1.8, ((0, 32), (1, 2), (2, 8)), jnp.float32),
        "cotangent": noise(streams_of[5], (TOKENS, D), 1.0, 6.0, ((0, 512),)),
        "weights": jnp.clip(0.05 + 0.25 * jax.random.uniform(streams_of[6], (TOKENS, TOP), jnp.float32) ** level_of(streams_of[6], (TOKENS, TOP), ((0, 512),), -0.2, 0.2), 0.05, 0.3),
        "expert_ids": draw_expert_ids(jax.random.fold_in(streams_of[10], 71), 0),
        "expert_counts": draw_expert_counts(jax.random.fold_in(streams_of[10], 71), 0),
        "hidden_saved": noise(streams_of[9], (N_ISLAND, N_DP, UNITS, SLOTS, FF_UNIT), 1.0, 6.0, ((0, 8), (1, 2), (2, 32))),
    }


beta_one = 0.9
beta_two = 0.95
adam_epsilon = 1e-08
inner_rate = 0.1
decay_rate = 0.1
outer_beta = 0.9
outer_rate = 0.7

def pack_rows(capacity, cotangent, weights, expert_ids, counts):
    window_experts = counts.shape[0]
    route_width = expert_ids.shape[1]
    flat_ids = expert_ids.reshape(-1)
    match_table = (flat_ids[:, None] == jnp.arange(window_experts, dtype=jnp.int32)[None, :]).astype(jnp.int32)
    earlier = jnp.cumsum(match_table, axis=0) - match_table
    pair_rank = lax.optimization_barrier(jnp.sum(earlier * match_table, axis=1))
    slot_limit = lax.optimization_barrier(jnp.sum(match_table * counts[None, :], axis=1))
    is_live = pair_rank < slot_limit
    slot_index = jnp.where(is_live, flat_ids * capacity + pair_rank, window_experts * capacity).astype(jnp.int32)
    source_row = (jnp.arange(flat_ids.shape[0], dtype=jnp.int32) // route_width).astype(jnp.int32)
    slot_source = jnp.zeros((window_experts * capacity + 1,), jnp.int32).at[slot_index].set(source_row)[:-1]
    live_weight = jnp.where(is_live, weights.reshape(-1), jnp.zeros_like(weights.reshape(-1)))
    slot_scale = jnp.zeros((window_experts * capacity + 1,), jnp.float32).at[slot_index].set(live_weight)[:-1]
    packed = (cotangent[slot_source].astype(jnp.float32) * slot_scale[:, None]).astype(jnp.bfloat16)
    return packed.reshape(window_experts, capacity, cotangent.shape[1])

def reference(theta, first_moment, second_moment, anchor, momentum, cotangent, weights, expert_ids, expert_counts, hidden_saved):
    scale = FF ** (-0.5)
    group_cot = cotangent.reshape(N_ISLAND, N_DP, N_EXPERT, TOK_DEV, D)
    group_weights = weights.reshape(N_ISLAND, N_DP, N_EXPERT, TOK_DEV, TOP)
    group_ids = expert_ids.reshape(N_ISLAND, N_DP, N_EXPERT, TOK_DEV, TOP)
    group_counts = expert_counts.reshape(N_ISLAND, N_DP, N_EXPERT, EXPERTS)
    packer = jax.vmap(pack_rows, in_axes=(None, 0, 0, 0, 0))

    def island_step(inputs):
        own_theta, own_first, own_second, own_cot, own_weights, own_ids, own_counts, own_saved = inputs
        grad = jnp.zeros((UNITS, FF_UNIT, D), jnp.float32)
        hidden_grads = []
        for data_index in range(N_DP):
            packed = packer(CAP, own_cot[data_index], own_weights[data_index], own_ids[data_index], own_counts[data_index])
            saved_group = own_saved[data_index]

            def unit_step(unit_index):
                chosen = lax.dynamic_index_in_dim(packed, unit_index // 2, 1, keepdims=False).reshape(SLOTS, D)
                saved = lax.dynamic_index_in_dim(saved_group, unit_index, 0, keepdims=False)
                weight_unit = lax.dynamic_index_in_dim(own_theta, unit_index, 0, keepdims=False)
                hidden_grad = (scale * jnp.dot(chosen, weight_unit.T, preferred_element_type=jnp.float32)).astype(jnp.bfloat16)
                partial_grad = (scale * jnp.dot(saved.T, chosen, preferred_element_type=jnp.float32)).astype(jnp.bfloat16)
                return (hidden_grad, partial_grad)
            hidden_part, partial_part = lax.map(unit_step, jnp.arange(UNITS, dtype=jnp.int32))
            partial_part = lax.optimization_barrier(partial_part)
            grad = grad + partial_part.astype(jnp.float32)
            hidden_grads.append(hidden_part)
        first_new = beta_one * own_first.astype(jnp.float32) + (1.0 - beta_one) * grad
        second_new = beta_two * own_second.astype(jnp.float32) + (1.0 - beta_two) * grad * grad
        theta_wide = own_theta.astype(jnp.float32)
        step_size = first_new / (jnp.sqrt(second_new) + adam_epsilon) + decay_rate * theta_wide
        theta_new = (theta_wide - inner_rate * step_size).astype(jnp.bfloat16)
        return (theta_new, jnp.stack(hidden_grads))
    new_thetas, d_hidden = lax.map(island_step, (theta, first_moment, second_moment, group_cot, group_weights, group_ids, group_counts, hidden_saved))
    delta_total = jnp.zeros_like(anchor)
    for island_index in range(N_ISLAND):
        delta_total = delta_total + (anchor - new_thetas[island_index].astype(jnp.float32))
    mean_delta = delta_total / N_ISLAND
    momentum_new = outer_beta * momentum + mean_delta
    anchor_new = anchor - outer_rate * (mean_delta + outer_beta * momentum_new)
    return (anchor_new, momentum_new, d_hidden)
```

```python
import functools

import jax
import jax.numpy as jnp
from jax import lax
from jax.experimental import pallas as pl
from jax.experimental.pallas import tpu as pltpu
from jax.sharding import PartitionSpec as P

FF = 768
CAP = 16
HALVES = 2
GROUPS = 2
AHEAD = 2

beta_one = 0.9
beta_two = 0.95
adam_epsilon = 1e-08
inner_rate = 0.1
decay_rate = 0.1
outer_beta = 0.9
outer_rate = 0.7

MESH = pl.DeviceIdType.MESH
F32 = jnp.float32
BF16 = jnp.bfloat16


def dot(a, b, dims):
    return lax.dot_general(a, b, (dims, ((), ())), preferred_element_type=F32)


def body(
    n_island,
    n_expert,
    ids_ref,
    weights_ref,
    counts_ref,
    theta_hbm,
    first_hbm,
    second_hbm,
    anchor_hbm,
    momentum_hbm,
    cot_hbm,
    saved_hbm,
    anchor_out,
    momentum_out,
    hidden_out,
    cot,
    saved,
    saved_t,
    first,
    second,
    anchor,
    momentum,
    picks,
    packed,
    slots,
    thetas,
    partial,
    partner_partial,
    new_theta,
    all_theta,
    hidden_acc,
    load_sem,
    saved_sem,
    theta_sem,
    send_sem,
    recv_sem,
    pass_send,
    pass_recv,
    theta_send,
    theta_recv,
    grad_send,
    grad_recv,
    island_send,
    island_recv,
):
    ring = n_expert // GROUPS
    pairs = ring // HALVES
    half_pairs = pairs // 2
    per_half = ring // HALVES
    experts = GROUPS * pairs
    rows = GROUPS * per_half * CAP
    width = cot.shape[1] // n_island
    theta_rows = thetas.shape[2]
    tokens = cot.shape[0]
    scale = FF ** (-0.5)

    island = lax.axis_index("island")
    dp = lax.axis_index("dp")
    me = lax.axis_index("expert")
    group = me // ring
    z = me % ring
    pair = z // HALVES
    half = z % HALVES
    partner = group * ring + pair * HALVES + (1 - half)
    other_dp = 1 - dp

    def columns(step):
        chunk = (island + 1 + step) % n_island
        return pl.ds(pl.multiple_of(chunk * width, width), width)

    loads = [
        pltpu.make_async_copy(src, dst, load_sem.at[k])
        for k, (src, dst) in enumerate(
            [
                (cot_hbm, cot),
                (first_hbm, first),
                (second_hbm, second),
                (anchor_hbm, anchor),
                (momentum_hbm, momentum),
            ]
        )
    ]
    loads[0].start()

    barrier = pltpu.get_barrier_semaphore()
    greeted = 0
    for other in range(GROUPS):
        for k in range(per_half):
            if other == 0 and k == 0:
                continue
            source_group = (group + other) % GROUPS
            source_z = (z + (2 * half - 1) * k + ring) % ring
            pl.semaphore_signal(
                barrier,
                inc=1,
                device_id={"expert": source_group * ring + source_z},
                device_id_type=MESH,
            )
            greeted += 1
    pl.semaphore_signal(barrier, inc=1, device_id={"expert": partner}, device_id_type=MESH)
    pl.semaphore_signal(barrier, inc=1, device_id={"dp": other_dp}, device_id_type=MESH)
    greeted += 2
    for k in range(1, n_island):
        pl.semaphore_signal(
            barrier, inc=1, device_id={"island": (island + k) % n_island}, device_id_type=MESH
        )
        greeted += 1

    def theta_load(step):
        return pltpu.make_async_copy(
            theta_hbm.at[:, columns(step)], thetas.at[step, dp], theta_sem.at[step]
        )

    for step in range(n_island):
        theta_load(step).start()

    def canonical(k):
        which = k // (GROUPS * per_half)
        other = (k // per_half) % GROUPS
        q = k % per_half
        source_z = (pair * HALVES - (per_half - 1) + per_half * which + q + ring) % ring
        return other * ring + source_z

    blocks = HALVES * GROUPS * per_half

    def load_saved(k, carry):
        pltpu.make_async_copy(
            saved_hbm.at[pl.ds(pl.multiple_of(canonical(k) * CAP, CAP), CAP)],
            saved.at[pl.ds(pl.multiple_of(k * CAP, CAP), CAP)],
            saved_sem,
        ).start()
        return carry

    lax.fori_loop(0, blocks, load_saved, 0)
    for load in loads[1:]:
        load.start()

    ids = ids_ref[...]
    weights = weights_ref[...]
    expert_of = lax.broadcasted_iota(jnp.int32, (experts, tokens), 0)
    named = jnp.zeros((experts, tokens), F32)
    weight = jnp.zeros((experts, tokens), F32)
    for k in range(ids.shape[0]):
        hit = ids[k : k + 1, :] == expert_of
        named = jnp.where(hit, 1.0, named)
        weight = jnp.where(hit, weights[k : k + 1, :], weight)
    before = (
        lax.broadcasted_iota(jnp.int32, (tokens, tokens), 0)
        < lax.broadcasted_iota(jnp.int32, (tokens, tokens), 1)
    )
    rank = dot(
        named.astype(BF16), jnp.where(before, 1.0, 0.0).astype(BF16), ((1,), (0,))
    ).astype(jnp.int32)
    diagonal = lax.broadcasted_iota(jnp.int32, (experts, experts), 0) == lax.broadcasted_iota(
        jnp.int32, (experts, experts), 1
    )
    count = jnp.sum(
        jnp.where(diagonal, counts_ref[...].astype(F32), 0.0), axis=1, keepdims=True
    ).astype(jnp.int32)
    rank = jnp.where((named > 0.0) & (rank < count), rank, CAP)
    slot_of = lax.broadcasted_iota(jnp.int32, (experts, CAP, tokens), 1)
    table = jnp.where(rank[:, None, :] == slot_of, weight[:, None, :], 0.0)
    table = table.reshape(experts * CAP, tokens)
    high = table.astype(BF16)
    rest = table - high.astype(F32)
    middle = rest.astype(BF16)
    picks[0] = high
    picks[1] = middle
    picks[2] = (rest - middle.astype(F32)).astype(BF16)

    own_row = (group * per_half + (1 - half) * (per_half - 1)) * CAP
    own_expert = group * pairs + pair

    def pack(step):
        chunk = cot[:, columns(step)]
        rows_out = sum(dot(picks[k], chunk, ((1,), (0,))) for k in range(3))
        packed[step] = rows_out.astype(BF16).reshape(experts, CAP, width)
        slots[step, half, pl.ds(pl.multiple_of(own_row, CAP), CAP), :] = packed[step, own_expert]

    def sends(step):
        copies = []
        for d in (half_pairs, *range(half_pairs - 1, 0, -1), *range(half_pairs + 1, pairs), 0):
            for other in range(GROUPS):
                if other == 0 and d == 0:
                    continue
                to_group = (group + other) % GROUPS
                to_pair = (pair + d) % pairs
                if d == 0:
                    to_half = half
                elif d == half_pairs:
                    to_half = 1 - half
                else:
                    to_half = 0 if d < half_pairs else 1
                place = (half - 2 * d + per_half - 1 - per_half * to_half + 3 * ring) % ring
                row = (group * per_half + place) * CAP
                copies.append(
                    pltpu.make_async_remote_copy(
                        packed.at[step, to_group * pairs + to_pair],
                        slots.at[step, to_half, pl.ds(pl.multiple_of(row, CAP), CAP)],
                        send_sem.at[step],
                        recv_sem.at[step],
                        device_id={"expert": to_group * ring + to_pair * HALVES + to_half},
                        device_id_type=MESH,
                    )
                )
        return copies

    def send(step):
        for copy in sends(step):
            copy.start()

    def arrived(step, sem):
        some = slots.at[step, 0, pl.ds(0, rows - CAP)]
        return pltpu.make_async_copy(some, some, sem.at[step])

    def pass_on(step):
        return pltpu.make_async_remote_copy(
            slots.at[step, half],
            slots.at[step, half],
            pass_send.at[step],
            pass_recv.at[step],
            device_id={"expert": partner},
            device_id_type=MESH,
        )

    def share_theta(step):
        return pltpu.make_async_remote_copy(
            thetas.at[step, dp],
            thetas.at[step, dp],
            theta_send.at[step],
            theta_recv.at[step],
            device_id={"dp": other_dp},
            device_id_type=MESH,
        )

    def share_grad(step):
        return pltpu.make_async_remote_copy(
            partial.at[step, other_dp],
            partner_partial.at[step],
            grad_send.at[step],
            grad_recv.at[step],
            device_id={"dp": other_dp},
            device_id_type=MESH,
        )

    def share_island(step):
        owner = (island + 1 + step) % n_island
        return pltpu.make_async_remote_copy(
            new_theta.at[step],
            all_theta.at[island],
            island_send.at[step],
            island_recv.at[island],
            device_id={"island": owner},
            device_id_type=MESH,
        )

    def contract(step):
        chunk = slots[step].reshape(HALVES * rows, width)
        product = (scale * dot(saved_t[...], chunk, ((1,), (0,)))).astype(BF16)
        partial[step, 0] = product[:theta_rows]
        partial[step, 1] = product[theta_rows:]
        share_grad(step).start()
        share_theta(step).wait_recv()
        full = thetas[step].reshape(2 * theta_rows, width)
        hidden_acc[...] += dot(chunk, full, ((1,), (1,)))

    def update(step):
        share_grad(step).wait_recv()
        grad = partial[step, dp].astype(F32) + partner_partial[step].astype(F32)
        first_new = beta_one * first[:, columns(step)].astype(F32) + (1.0 - beta_one) * grad
        second_new = (
            beta_two * second[:, columns(step)].astype(F32) + (1.0 - beta_two) * grad * grad
        )
        wide = thetas[step, dp].astype(F32)
        step_size = first_new / (jnp.sqrt(second_new) + adam_epsilon) + decay_rate * wide
        return (wide - inner_rate * step_size).astype(BF16)

    loads[0].wait()
    for step in range(AHEAD):
        pack(step)

    pl.semaphore_wait(barrier, greeted)
    for step in range(AHEAD):
        send(step)

    for step in range(n_island):
        theta_load(step).wait()
        share_theta(step).start()

    pltpu.make_async_copy(saved, saved, saved_sem).wait()
    saved_t[...] = saved[...].T
    hidden_acc[...] = jnp.zeros_like(hidden_acc)
    for load in loads[1:]:
        load.wait()

    def run(t, carry):
        @pl.when(t + AHEAD < n_island)
        def _():
            pack(t + AHEAD)
            send(t + AHEAD)

        @pl.when(t < n_island)
        def _():
            arrived(t, recv_sem).wait()
            pass_on(t).start()

        @pl.when((t >= 1) & (t <= n_island))
        def _():
            pass_on(t - 1).wait_recv()
            contract(t - 1)

        @pl.when(t >= 2)
        def _():
            fresh = update(t - 2)

            @pl.when(t < n_island + 1)
            def _():
                new_theta[t - 2] = fresh
                share_island(t - 2).start()

            @pl.when(t == n_island + 1)
            def _():
                all_theta[island] = fresh

        return carry

    lax.fori_loop(0, n_island + 2, run, 0)

    for k in range(blocks):
        at = pl.ds(pl.multiple_of(canonical(k) * CAP, CAP), CAP)
        hidden_out[at, :] = (scale * hidden_acc[k * CAP : (k + 1) * CAP, :]).astype(BF16)

    for k in range(1, n_island):
        source = (island + k) % n_island
        pltpu.make_async_copy(
            all_theta.at[source], all_theta.at[source], island_recv.at[source]
        ).wait()
    total = all_theta[0].astype(F32)
    for k in range(1, n_island):
        total += all_theta[k].astype(F32)
    mean_delta = anchor[...] - total / n_island
    momentum_new = outer_beta * momentum[...] + mean_delta
    momentum_out[...] = momentum_new
    anchor_out[...] = anchor[...] - outer_rate * (mean_delta + outer_beta * momentum_new)

    for step in range(n_island):
        arrived(step, send_sem).wait()
        pass_on(step).wait_send()
        share_theta(step).wait_send()
        share_grad(step).wait_send()
        if step < n_island - 1:
            share_island(step).wait_send()


def per_device(
    n_island,
    n_expert,
    theta,
    first_moment,
    second_moment,
    anchor,
    momentum,
    cotangent,
    weights,
    expert_ids,
    expert_counts,
    hidden_saved,
):
    n = n_island
    theta_rows, features = theta.shape[2:]
    width = features // n
    slots, units = hidden_saved.shape[3:]
    experts = n_expert // HALVES
    tokens = cotangent.shape[0]
    dma = pltpu.SemaphoreType.DMA
    vmem = pl.BlockSpec(memory_space=pltpu.VMEM)
    hbm = pl.BlockSpec(memory_space=pl.ANY)
    anchor_new, momentum_new, d_hidden = pl.pallas_call(
        functools.partial(body, n_island, n_expert),
        out_shape=(
            jax.ShapeDtypeStruct((theta_rows, width), F32),
            jax.ShapeDtypeStruct((theta_rows, width), F32),
            jax.ShapeDtypeStruct((slots, units), BF16),
        ),
        in_specs=[vmem] * 3 + [hbm] * 7,
        out_specs=(vmem,) * 3,
        scratch_shapes=[
            pltpu.VMEM((tokens, features), BF16),
            pltpu.VMEM((slots, units), BF16),
            pltpu.VMEM((units, slots), BF16),
            pltpu.VMEM((theta_rows, features), BF16),
            pltpu.VMEM((theta_rows, features), BF16),
            pltpu.VMEM((theta_rows, width), F32),
            pltpu.VMEM((theta_rows, width), F32),
            pltpu.VMEM((3, experts * CAP, tokens), BF16),
            pltpu.VMEM((n, experts, CAP, width), BF16),
            pltpu.VMEM((n, HALVES, slots // HALVES, width), BF16),
            pltpu.VMEM((n, 2, theta_rows, width), BF16),
            pltpu.VMEM((n, 2, theta_rows, width), BF16),
            pltpu.VMEM((n, theta_rows, width), BF16),
            pltpu.VMEM((n, theta_rows, width), BF16),
            pltpu.VMEM((n, theta_rows, width), BF16),
            pltpu.VMEM((slots, units), F32),
            dma((5,)),
            dma,
            dma((n,)),
            dma((n,)),
            dma((n,)),
            dma((n,)),
            dma((n,)),
            dma((n,)),
            dma((n,)),
            dma((n,)),
            dma((n,)),
            dma((n,)),
            dma((n,)),
        ],
        compiler_params=pltpu.CompilerParams(
            collective_id=0, has_side_effects=True, vmem_limit_bytes=48 << 20
        ),
        name="diloco_step",
    )(
        expert_ids.T,
        weights.T,
        expert_counts,
        theta.reshape(theta_rows, features),
        first_moment.reshape(theta_rows, features),
        second_moment.reshape(theta_rows, features),
        anchor.reshape(theta_rows, width),
        momentum.reshape(theta_rows, width),
        cotangent,
        hidden_saved.reshape(slots, units),
    )
    return (
        anchor_new.reshape(anchor.shape),
        momentum_new.reshape(momentum.shape),
        d_hidden.reshape(hidden_saved.shape),
    )


def solution(mesh):
    return jax.shard_map(
        functools.partial(per_device, mesh.shape["island"], mesh.shape["expert"]),
        mesh=mesh,
        in_specs=(
            P("island", "expert", "dp", None),
            P("island", "expert", "dp", None),
            P("island", "expert", "dp", None),
            P("expert", "dp", "island"),
            P("expert", "dp", "island"),
            P(("island", "dp", "expert"), None),
            P(("island", "dp", "expert"), None),
            P(("island", "dp", "expert"), None),
            P(("island", "dp", "expert"), None),
            P("island", "dp", "expert", None, None),
        ),
        out_specs=(
            P("expert", "dp", "island"),
            P("expert", "dp", "island"),
            P("island", "dp", "expert", None, None),
        ),
        check_vma=False,
    )
```

```python
import functools

import jax
import jax.numpy as jnp
from jax import lax
from jax.experimental import pallas as pl
from jax.experimental.pallas import tpu as pltpu
from jax.sharding import PartitionSpec as P

FF = 768
CAP = 16
HALVES = 2
GROUPS = 2
LAST = 1
AHEAD = 3

beta_one = 0.9
beta_two = 0.95
adam_epsilon = 1e-08
inner_rate = 0.1
decay_rate = 0.1
outer_beta = 0.9
outer_rate = 0.7

VMEM_LIMIT = 48 << 20
MESH = pl.DeviceIdType.MESH
F32 = jnp.float32
BF16 = jnp.bfloat16


def dot(a, b, dims):
    return lax.dot_general(a, b, (dims, ((), ())), preferred_element_type=F32)


def body(
    n_island,
    n_expert,
    ids_hbm,
    weights_hbm,
    counts_hbm,
    theta_hbm,
    first_hbm,
    second_hbm,
    anchor_hbm,
    momentum_hbm,
    cot_hbm,
    saved_hbm,
    anchor_out,
    momentum_out,
    hidden_out,
    ids_ref,
    weights_ref,
    counts_ref,
    cot,
    saved,
    saved_t,
    first,
    second,
    anchor,
    momentum,
    picks,
    packed,
    packed_last,
    slots,
    slots_last,
    thetas,
    thetas_last,
    partial,
    partial_last,
    partner_partial,
    partner_partial_last,
    new_theta,
    all_theta,
    hidden_acc,
    load_sem,
    saved_sem,
    theta_sem,
    send_sem,
    recv_sem,
    pass_send,
    pass_recv,
    theta_send,
    theta_recv,
    grad_send,
    grad_recv,
    island_send,
    island_recv,
):
    ring = n_expert // GROUPS
    pairs = ring // HALVES
    half_pairs = pairs // 2
    per_half = ring // HALVES
    experts = GROUPS * pairs
    rows = GROUPS * per_half * CAP
    away = n_island - 1
    steps = away + LAST
    share = cot.shape[1] // n_island
    narrow = share // LAST
    theta_rows = thetas.shape[2]
    tokens = cot.shape[0]
    scale = FF ** (-0.5)

    island = lax.axis_index("island")
    dp = lax.axis_index("dp")
    me = lax.axis_index("expert")
    group = me // ring
    z = me % ring
    pair = z // HALVES
    half = z % HALVES
    partner = group * ring + pair * HALVES + (1 - half)
    other_dp = 1 - dp

    def last(step):
        return isinstance(step, int) and step >= away

    def columns(step):
        if last(step):
            start = island * share + (step - away) * narrow
            return pl.ds(pl.multiple_of(start, narrow), narrow)
        return pl.ds(pl.multiple_of((island + 1 + step) % n_island * share, share), share)

    def of(wide, cut, step):
        return cut.at[step - away] if last(step) else wide.at[step]

    loads = [
        pltpu.make_async_copy(src, dst, load_sem.at[k])
        for k, (src, dst) in enumerate(
            [
                (ids_hbm, ids_ref),
                (weights_hbm, weights_ref),
                (counts_hbm, counts_ref),
                (cot_hbm, cot),
                (first_hbm, first),
                (second_hbm, second),
                (anchor_hbm, anchor),
                (momentum_hbm, momentum),
            ]
        )
    ]
    for load in loads[:4]:
        load.start()

    barrier = pltpu.get_barrier_semaphore()
    greeted = 0
    for other in range(GROUPS):
        for k in range(per_half):
            if other == 0 and k == 0:
                continue
            source_group = (group + other) % GROUPS
            source_z = (z + (2 * half - 1) * k + ring) % ring
            pl.semaphore_signal(
                barrier,
                inc=1,
                device_id={"expert": source_group * ring + source_z},
                device_id_type=MESH,
            )
            greeted += 1
    pl.semaphore_signal(barrier, inc=1, device_id={"expert": partner}, device_id_type=MESH)
    pl.semaphore_signal(barrier, inc=1, device_id={"dp": other_dp}, device_id_type=MESH)
    greeted += 2
    for k in range(1, n_island):
        pl.semaphore_signal(
            barrier, inc=1, device_id={"island": (island + k) % n_island}, device_id_type=MESH
        )
        greeted += 1

    def theta_load(step):
        return pltpu.make_async_copy(
            theta_hbm.at[:, columns(step)], of(thetas, thetas_last, step).at[dp], theta_sem.at[step]
        )

    def canonical(k):
        which = k // (GROUPS * per_half)
        other = (k // per_half) % GROUPS
        q = k % per_half
        source_z = (pair * HALVES - (per_half - 1) + per_half * which + q + ring) % ring
        return other * ring + source_z

    blocks = HALVES * GROUPS * per_half

    def load_saved(k, carry):
        pltpu.make_async_copy(
            saved_hbm.at[pl.ds(pl.multiple_of(canonical(k) * CAP, CAP), CAP)],
            saved.at[pl.ds(pl.multiple_of(k * CAP, CAP), CAP)],
            saved_sem,
        ).start()
        return carry

    for load in loads[:3]:
        load.wait()
    ids = ids_ref[...]
    weights = weights_ref[...]
    expert_of = lax.broadcasted_iota(jnp.int32, (experts, tokens), 0)
    named = jnp.zeros((experts, tokens), F32)
    weight = jnp.zeros((experts, tokens), F32)
    for k in range(ids.shape[0]):
        hit = ids[k : k + 1, :] == expert_of
        named = jnp.where(hit, 1.0, named)
        weight = jnp.where(hit, weights[k : k + 1, :], weight)
    before = (
        lax.broadcasted_iota(jnp.int32, (tokens, tokens), 0)
        < lax.broadcasted_iota(jnp.int32, (tokens, tokens), 1)
    )
    rank = dot(
        named.astype(BF16), jnp.where(before, 1.0, 0.0).astype(BF16), ((1,), (0,))
    ).astype(jnp.int32)
    diagonal = lax.broadcasted_iota(jnp.int32, (experts, experts), 0) == lax.broadcasted_iota(
        jnp.int32, (experts, experts), 1
    )
    count = jnp.sum(
        jnp.where(diagonal, counts_ref[...].astype(F32), 0.0), axis=1, keepdims=True
    ).astype(jnp.int32)
    rank = jnp.where((named > 0.0) & (rank < count), rank, CAP)
    slot_of = lax.broadcasted_iota(jnp.int32, (experts, CAP, tokens), 1)
    table = jnp.where(rank[:, None, :] == slot_of, weight[:, None, :], 0.0)
    table = table.reshape(experts * CAP, tokens)
    high = table.astype(BF16)
    rest = table - high.astype(F32)
    middle = rest.astype(BF16)
    picks[0] = high
    picks[1] = middle
    picks[2] = (rest - middle.astype(F32)).astype(BF16)

    own_row = (group * per_half + (1 - half) * (per_half - 1)) * CAP
    own_expert = group * pairs + pair

    def pack(step):
        chunk = cot[:, columns(step)]
        rows_out = sum(dot(picks[k], chunk, ((1,), (0,))) for k in range(3))
        to = of(packed, packed_last, step)
        to[...] = rows_out.astype(BF16).reshape(experts, CAP, -1)
        own = of(slots, slots_last, step).at[half, pl.ds(pl.multiple_of(own_row, CAP), CAP)]
        own[...] = to[own_expert]

    def sends(step):
        copies = []
        for d in (half_pairs, *range(half_pairs - 1, 0, -1), *range(half_pairs + 1, pairs), 0):
            for other in range(GROUPS):
                if other == 0 and d == 0:
                    continue
                to_group = (group + other) % GROUPS
                to_pair = (pair + d) % pairs
                if d == 0:
                    to_half = half
                elif d == half_pairs:
                    to_half = 1 - half
                else:
                    to_half = 0 if d < half_pairs else 1
                place = (half - 2 * d + per_half - 1 - per_half * to_half + 3 * ring) % ring
                row = (group * per_half + place) * CAP
                copies.append(
                    pltpu.make_async_remote_copy(
                        of(packed, packed_last, step).at[to_group * pairs + to_pair],
                        of(slots, slots_last, step).at[
                            to_half, pl.ds(pl.multiple_of(row, CAP), CAP)
                        ],
                        send_sem.at[step],
                        recv_sem.at[step],
                        device_id={"expert": to_group * ring + to_pair * HALVES + to_half},
                        device_id_type=MESH,
                    )
                )
        return copies

    def send(step):
        for copy in sends(step):
            copy.start()

    def arrived(step, sem):
        some = of(slots, slots_last, step).at[0, pl.ds(0, rows - CAP)]
        return pltpu.make_async_copy(some, some, sem.at[step])

    def pass_on(step):
        return pltpu.make_async_remote_copy(
            of(slots, slots_last, step).at[half],
            of(slots, slots_last, step).at[half],
            pass_send.at[step],
            pass_recv.at[step],
            device_id={"expert": partner},
            device_id_type=MESH,
        )

    def share_theta(step):
        return pltpu.make_async_remote_copy(
            of(thetas, thetas_last, step).at[dp],
            of(thetas, thetas_last, step).at[dp],
            theta_send.at[step],
            theta_recv.at[step],
            device_id={"dp": other_dp},
            device_id_type=MESH,
        )

    def share_grad(step):
        return pltpu.make_async_remote_copy(
            of(partial, partial_last, step).at[other_dp],
            of(partner_partial, partner_partial_last, step),
            grad_send.at[step],
            grad_recv.at[step],
            device_id={"dp": other_dp},
            device_id_type=MESH,
        )

    def share_island(step):
        owner = (island + 1 + step) % n_island
        return pltpu.make_async_remote_copy(
            new_theta.at[step],
            all_theta.at[island],
            island_send.at[step],
            island_recv.at[island],
            device_id={"island": owner},
            device_id_type=MESH,
        )

    def contract(step):
        pass_on(step).wait_recv()
        chunk = of(slots, slots_last, step)[...].reshape(HALVES * rows, -1)
        product = (scale * dot(saved_t[...], chunk, ((1,), (0,)))).astype(BF16)
        to = of(partial, partial_last, step)
        to[0] = product[:theta_rows]
        to[1] = product[theta_rows:]
        share_grad(step).start()
        share_theta(step).wait_recv()
        full = of(thetas, thetas_last, step)[...].reshape(2 * theta_rows, -1)
        hidden_acc[...] += dot(chunk, full, ((1,), (1,)))

    def update(step):
        share_grad(step).wait_recv()
        mine = of(partial, partial_last, step)[dp].astype(F32)
        grad = mine + of(partner_partial, partner_partial_last, step)[...].astype(F32)
        first_new = beta_one * first[:, columns(step)].astype(F32) + (1.0 - beta_one) * grad
        second_new = (
            beta_two * second[:, columns(step)].astype(F32) + (1.0 - beta_two) * grad * grad
        )
        wide = of(thetas, thetas_last, step)[dp].astype(F32)
        step_size = first_new / (jnp.sqrt(second_new) + adam_epsilon) + decay_rate * wide
        return (wide - inner_rate * step_size).astype(BF16)

    def update_away(step):
        new_theta[step] = update(step)
        share_island(step).start()

    loads[3].wait()
    pack(0)
    pl.semaphore_wait(barrier, greeted)
    send(0)
    for step in range(1, min(AHEAD, steps)):
        pack(step)
        send(step)

    for step in range(steps):
        theta_load(step).start()
    lax.fori_loop(0, blocks, load_saved, 0)
    for load in loads[4:]:
        load.start()
    hidden_acc[...] = jnp.zeros_like(hidden_acc)
    for step in range(steps):
        theta_load(step).wait()
    for step in range(min(AHEAD, steps)):
        share_theta(step).start()
    pltpu.make_async_copy(saved, saved, saved_sem).wait()
    saved_t[...] = saved[...].T
    for load in loads[4:]:
        load.wait()

    def pass_along(step):
        arrived(step, recv_sem).wait()
        pass_on(step).start()

    def advance(step):
        share_theta(step).start()
        pack(step)
        send(step)

    def run(t, carry):
        pass_along(t)

        @pl.when(t + AHEAD < away)
        def _():
            advance(t + AHEAD)

        for step in range(away, steps):

            @pl.when(t + AHEAD == step)
            def _():
                advance(step)

        @pl.when(t >= 1)
        def _():
            contract(t - 1)

        @pl.when(t >= 2)
        def _():
            update_away(t - 2)

        return carry

    lax.fori_loop(0, away, run, 0)
    for step in range(away + AHEAD, steps):
        advance(step)

    pass_along(away)
    contract(away - 1)
    if away >= 2:
        update_away(away - 2)
    for step in range(away + 1, steps):
        pass_along(step)
    update_away(away - 1)
    for step in range(away, steps):
        contract(step)

    others = jnp.zeros((theta_rows, share), F32)
    for hop in range(1, n_island):
        source = (island + hop) % n_island
        landed = all_theta.at[source]
        pltpu.make_async_copy(landed, landed, island_recv.at[source]).wait()
        others += landed[...].astype(F32)

    for k in range(blocks):
        at = pl.ds(pl.multiple_of(canonical(k) * CAP, CAP), CAP)
        hidden_out[at, :] = (scale * hidden_acc[k * CAP : (k + 1) * CAP, :]).astype(BF16)

    for step in range(away, steps):
        at = slice((step - away) * narrow, (step - away + 1) * narrow)
        mean_delta = anchor[:, at] - (others[:, at] + update(step).astype(F32)) / n_island
        momentum_new = outer_beta * momentum[:, at] + mean_delta
        momentum_out[:, at] = momentum_new
        anchor_out[:, at] = anchor[:, at] - outer_rate * (mean_delta + outer_beta * momentum_new)

    for step in range(steps):
        arrived(step, send_sem).wait()
        pass_on(step).wait_send()
        share_theta(step).wait_send()
        share_grad(step).wait_send()
        if step < away:
            share_island(step).wait_send()


def store(anchor, momentum, hidden, anchor_hbm, momentum_hbm, hidden_hbm, sems):
    copies = [
        pltpu.make_async_copy(src, dst, sems.at[k])
        for k, (src, dst) in enumerate(
            [(anchor, anchor_hbm), (momentum, momentum_hbm), (hidden, hidden_hbm)]
        )
    ]
    for copy in copies:
        copy.start()
    for copy in copies:
        copy.wait()


def per_device(
    n_island,
    n_expert,
    theta,
    first_moment,
    second_moment,
    anchor,
    momentum,
    cotangent,
    weights,
    expert_ids,
    expert_counts,
    hidden_saved,
):
    away = n_island - 1
    steps = away + LAST
    theta_rows, features = theta.shape[2:]
    share = features // n_island
    narrow = share // LAST
    slots, units = hidden_saved.shape[3:]
    experts = n_expert // HALVES
    tokens, top = expert_ids.shape
    dma = pltpu.SemaphoreType.DMA

    def both(*shape):
        return (
            pltpu.VMEM((away, *shape, share), BF16),
            pltpu.VMEM((LAST, *shape, narrow), BF16),
        )

    vmem = pl.BlockSpec(memory_space=pltpu.VMEM)
    hbm = pl.BlockSpec(memory_space=pltpu.HBM)
    results = (
        jax.ShapeDtypeStruct((theta_rows, share), F32),
        jax.ShapeDtypeStruct((theta_rows, share), F32),
        jax.ShapeDtypeStruct((slots, units), BF16),
    )
    fresh = pl.pallas_call(
        functools.partial(body, n_island, n_expert),
        out_shape=results,
        in_specs=[hbm] * 10,
        out_specs=(vmem,) * 3,
        scratch_shapes=[
            pltpu.VMEM((top, tokens), jnp.int32),
            pltpu.VMEM((top, tokens), F32),
            pltpu.VMEM((1, experts), jnp.int32),
            pltpu.VMEM((tokens, features), BF16),
            pltpu.VMEM((slots, units), BF16),
            pltpu.VMEM((units, slots), BF16),
            pltpu.VMEM((theta_rows, features), BF16),
            pltpu.VMEM((theta_rows, features), BF16),
            pltpu.VMEM((theta_rows, share), F32),
            pltpu.VMEM((theta_rows, share), F32),
            pltpu.VMEM((3, experts * CAP, tokens), BF16),
            *both(experts, CAP),
            *both(HALVES, slots // HALVES),
            *both(2, theta_rows),
            *both(2, theta_rows),
            *both(theta_rows),
            pltpu.VMEM((away, theta_rows, share), BF16),
            pltpu.VMEM((n_island, theta_rows, share), BF16),
            pltpu.VMEM((slots, units), F32),
            dma((8,)),
            dma,
            dma((steps,)),
            dma((steps,)),
            dma((steps,)),
            dma((steps,)),
            dma((steps,)),
            dma((steps,)),
            dma((steps,)),
            dma((steps,)),
            dma((steps,)),
            dma((steps,)),
            dma((n_island,)),
        ],
        compiler_params=pltpu.CompilerParams(
            collective_id=0, has_side_effects=True, vmem_limit_bytes=VMEM_LIMIT
        ),
        name="diloco_step",
    )(
        *(
            pltpu.with_memory_space_constraint(x, pltpu.HBM)
            for x in (
                expert_ids.T,
                weights.T,
                expert_counts,
                theta.reshape(theta_rows, features),
                first_moment.reshape(theta_rows, features),
                second_moment.reshape(theta_rows, features),
                anchor.reshape(theta_rows, share),
                momentum.reshape(theta_rows, share),
                cotangent,
                hidden_saved.reshape(slots, units),
            )
        )
    )
    anchor_new, momentum_new, d_hidden = pl.pallas_call(
        store,
        out_shape=results,
        in_specs=[vmem] * 3,
        out_specs=(hbm,) * 3,
        scratch_shapes=[dma((3,))],
        name="store",
    )(*(pltpu.with_memory_space_constraint(x, pltpu.VMEM) for x in fresh))
    return (
        anchor_new.reshape(anchor.shape),
        momentum_new.reshape(momentum.shape),
        d_hidden.reshape(hidden_saved.shape),
    )


def solution(mesh):
    return jax.shard_map(
        functools.partial(per_device, mesh.shape["island"], mesh.shape["expert"]),
        mesh=mesh,
        in_specs=(
            P("island", "expert", "dp", None),
            P("island", "expert", "dp", None),
            P("island", "expert", "dp", None),
            P("expert", "dp", "island"),
            P("expert", "dp", "island"),
            P(("island", "dp", "expert"), None),
            P(("island", "dp", "expert"), None),
            P(("island", "dp", "expert"), None),
            P(("island", "dp", "expert"), None),
            P("island", "dp", "expert", None, None),
        ),
        out_specs=(
            P("expert", "dp", "island"),
            P("expert", "dp", "island"),
            P("island", "dp", "expert", None, None),
        ),
        check_vma=False,
    )
```

```python
import functools

import jax
import jax.numpy as jnp
from jax import lax
from jax.experimental import pallas as pl
from jax.experimental.pallas import tpu as pltpu
from jax.sharding import PartitionSpec as P

FF = 768
CAP = 16
CORES = 2
HALVES = 2
GROUPS = 2
LAST = 1
AHEAD = 3
AHEAD_LAST = 3

beta_one = 0.9
beta_two = 0.95
adam_epsilon = 1e-08
inner_rate = 0.1
decay_rate = 0.1
outer_beta = 0.9
outer_rate = 0.7

VMEM_LIMIT = 48 << 20
MESH = pl.DeviceIdType.MESH
F32 = jnp.float32
BF16 = jnp.bfloat16


def dot(a, b, dims):
    return lax.dot_general(a, b, (dims, ((), ())), preferred_element_type=F32)


def body(
    n_island,
    n_expert,
    ids_hbm,
    weights_hbm,
    counts_hbm,
    theta_hbm,
    first_hbm,
    second_hbm,
    anchor_hbm,
    momentum_hbm,
    cot_hbm,
    saved_hbm,
    anchor_out,
    momentum_out,
    hidden_out,
    ids_ref,
    weights_ref,
    counts_ref,
    cot,
    saved,
    saved_t,
    first,
    second,
    anchor,
    momentum,
    picks,
    packed,
    packed_last,
    slots,
    slots_last,
    thetas,
    thetas_last,
    partial,
    partial_last,
    partner_partial,
    partner_partial_last,
    new_theta,
    all_theta,
    hidden_acc,
    load_sem,
    saved_sem,
    theta_sem,
    send_sem,
    recv_sem,
    pass_send,
    pass_recv,
    theta_send,
    theta_recv,
    grad_send,
    grad_recv,
    island_send,
    island_recv,
):
    ring = n_expert // GROUPS
    pairs = ring // HALVES
    half_pairs = pairs // 2
    per_half = ring // HALVES
    experts = GROUPS * pairs
    rows = GROUPS * per_half * CAP
    away = n_island - 1
    steps = away + LAST
    share = cot.shape[1] // n_island
    narrow = share // LAST
    theta_rows = thetas.shape[2]
    tokens = cot.shape[0]
    scale = FF ** (-0.5)

    island = lax.axis_index("island")
    dp = lax.axis_index("dp")
    me = lax.axis_index("expert")
    group = me // ring
    z = me % ring
    pair = z // HALVES
    half = z % HALVES
    partner = group * ring + pair * HALVES + (1 - half)
    other_dp = 1 - dp

    def owner_of(step):
        apart = n_island - 1 - step
        chip = (island // CORES + apart // CORES) % (n_island // CORES)
        return chip * CORES + (island % CORES + apart % CORES) % CORES

    def last(step):
        return isinstance(step, int) and step >= away

    def columns(step):
        if last(step):
            start = island * share + (step - away) * narrow
            return pl.ds(pl.multiple_of(start, narrow), narrow)
        return pl.ds(pl.multiple_of(owner_of(step) * share, share), share)

    def of(wide, cut, step):
        return cut.at[step - away] if last(step) else wide.at[step]

    loads = [
        pltpu.make_async_copy(src, dst, load_sem.at[k])
        for k, (src, dst) in enumerate(
            [
                (ids_hbm, ids_ref),
                (weights_hbm, weights_ref),
                (counts_hbm, counts_ref),
                (cot_hbm, cot),
                (first_hbm, first),
                (second_hbm, second),
                (anchor_hbm, anchor),
                (momentum_hbm, momentum),
            ]
        )
    ]

    barrier = pltpu.get_barrier_semaphore()
    greeted = 0
    for other in range(GROUPS):
        for k in range(per_half):
            if other == 0 and k == 0:
                continue
            source_group = (group + other) % GROUPS
            source_z = (z + (2 * half - 1) * k + ring) % ring
            pl.semaphore_signal(
                barrier,
                inc=1,
                device_id={"expert": source_group * ring + source_z},
                device_id_type=MESH,
            )
            greeted += 1
    pl.semaphore_signal(barrier, inc=1, device_id={"expert": partner}, device_id_type=MESH)
    pl.semaphore_signal(barrier, inc=1, device_id={"dp": other_dp}, device_id_type=MESH)
    greeted += 2
    for k in range(1, n_island):
        pl.semaphore_signal(
            barrier, inc=1, device_id={"island": (island + k) % n_island}, device_id_type=MESH
        )
        greeted += 1

    for load in loads[:4]:
        load.start()

    def theta_load(step):
        return pltpu.make_async_copy(
            theta_hbm.at[:, columns(step)], of(thetas, thetas_last, step).at[dp], theta_sem.at[step]
        )

    def canonical(k):
        which = k // (GROUPS * per_half)
        other = (k // per_half) % GROUPS
        q = k % per_half
        source_z = (pair * HALVES - (per_half - 1) + per_half * which + q + ring) % ring
        return other * ring + source_z

    blocks = HALVES * GROUPS * per_half

    def load_saved(k, carry):
        pltpu.make_async_copy(
            saved_hbm.at[pl.ds(pl.multiple_of(canonical(k) * CAP, CAP), CAP)],
            saved.at[pl.ds(pl.multiple_of(k * CAP, CAP), CAP)],
            saved_sem,
        ).start()
        return carry

    for load in loads[:3]:
        load.wait()
    ids = ids_ref[...]
    weights = weights_ref[...]
    expert_of = lax.broadcasted_iota(jnp.int32, (experts, tokens), 0)
    named = jnp.zeros((experts, tokens), F32)
    weight = jnp.zeros((experts, tokens), F32)
    for k in range(ids.shape[0]):
        hit = ids[k : k + 1, :] == expert_of
        named = jnp.where(hit, 1.0, named)
        weight = jnp.where(hit, weights[k : k + 1, :], weight)
    before = (
        lax.broadcasted_iota(jnp.int32, (tokens, tokens), 0)
        < lax.broadcasted_iota(jnp.int32, (tokens, tokens), 1)
    )
    rank = dot(
        named.astype(BF16), jnp.where(before, 1.0, 0.0).astype(BF16), ((1,), (0,))
    ).astype(jnp.int32)
    diagonal = lax.broadcasted_iota(jnp.int32, (experts, experts), 0) == lax.broadcasted_iota(
        jnp.int32, (experts, experts), 1
    )
    count = jnp.sum(
        jnp.where(diagonal, counts_ref[...].astype(F32), 0.0), axis=1, keepdims=True
    ).astype(jnp.int32)
    rank = jnp.where((named > 0.0) & (rank < count), rank, CAP)
    slot_of = lax.broadcasted_iota(jnp.int32, (experts, CAP, tokens), 1)
    table = jnp.where(rank[:, None, :] == slot_of, weight[:, None, :], 0.0)
    table = table.reshape(experts * CAP, tokens)
    high = table.astype(BF16)
    rest = table - high.astype(F32)
    middle = rest.astype(BF16)
    picks[0] = high
    picks[1] = middle
    picks[2] = (rest - middle.astype(F32)).astype(BF16)

    own_row = (group * per_half + (1 - half) * (per_half - 1)) * CAP
    own_expert = group * pairs + pair

    def pack(step):
        chunk = cot[:, columns(step)]
        rows_out = sum(dot(picks[k], chunk, ((1,), (0,))) for k in range(3))
        to = of(packed, packed_last, step)
        to[...] = rows_out.astype(BF16).reshape(experts, CAP, -1)
        own = of(slots, slots_last, step).at[half, pl.ds(pl.multiple_of(own_row, CAP), CAP)]
        own[...] = to[own_expert]

    def sends(step):
        copies = []
        for d in (half_pairs, *range(half_pairs - 1, 0, -1), *range(half_pairs + 1, pairs), 0):
            for other in range(GROUPS):
                if other == 0 and d == 0:
                    continue
                to_group = (group + other) % GROUPS
                to_pair = (pair + d) % pairs
                if d == 0:
                    to_half = half
                elif d == half_pairs:
                    to_half = 1 - half
                else:
                    to_half = 0 if d < half_pairs else 1
                place = (half - 2 * d + per_half - 1 - per_half * to_half + 3 * ring) % ring
                row = (group * per_half + place) * CAP
                copies.append(
                    pltpu.make_async_remote_copy(
                        of(packed, packed_last, step).at[to_group * pairs + to_pair],
                        of(slots, slots_last, step).at[
                            to_half, pl.ds(pl.multiple_of(row, CAP), CAP)
                        ],
                        send_sem.at[step],
                        recv_sem.at[step],
                        device_id={"expert": to_group * ring + to_pair * HALVES + to_half},
                        device_id_type=MESH,
                    )
                )
        return copies

    def send(step):
        for copy in sends(step):
            copy.start()

    def arrived(step, sem):
        some = of(slots, slots_last, step).at[0, pl.ds(0, rows - CAP)]
        return pltpu.make_async_copy(some, some, sem.at[step])

    def pass_on(step):
        return pltpu.make_async_remote_copy(
            of(slots, slots_last, step).at[half],
            of(slots, slots_last, step).at[half],
            pass_send.at[step],
            pass_recv.at[step],
            device_id={"expert": partner},
            device_id_type=MESH,
        )

    def share_theta(step):
        return pltpu.make_async_remote_copy(
            of(thetas, thetas_last, step).at[dp],
            of(thetas, thetas_last, step).at[dp],
            theta_send.at[step],
            theta_recv.at[step],
            device_id={"dp": other_dp},
            device_id_type=MESH,
        )

    def share_grad(step):
        return pltpu.make_async_remote_copy(
            of(partial, partial_last, step).at[other_dp],
            of(partner_partial, partner_partial_last, step),
            grad_send.at[step],
            grad_recv.at[step],
            device_id={"dp": other_dp},
            device_id_type=MESH,
        )

    def share_island(step):
        owner = owner_of(step)
        return pltpu.make_async_remote_copy(
            new_theta.at[step],
            all_theta.at[island],
            island_send.at[step],
            island_recv.at[island],
            device_id={"island": owner},
            device_id_type=MESH,
        )

    def contract(step):
        pass_on(step).wait_recv()
        chunk = of(slots, slots_last, step)[...].reshape(HALVES * rows, -1)
        to = of(partial, partial_last, step)

        def product(part):
            at = pl.ds(pl.multiple_of(part * theta_rows, theta_rows), theta_rows)
            return (scale * dot(saved_t[at, :], chunk, ((1,), (0,)))).astype(BF16)

        to[other_dp] = product(other_dp)
        share_grad(step).start()
        to[dp] = product(dp)
        share_theta(step).wait_recv()
        full = of(thetas, thetas_last, step)[...].reshape(2 * theta_rows, -1)
        hidden_acc[...] += dot(chunk, full, ((1,), (1,)))

    def update(step):
        share_grad(step).wait_recv()
        mine = of(partial, partial_last, step)[dp].astype(F32)
        grad = mine + of(partner_partial, partner_partial_last, step)[...].astype(F32)
        first_new = beta_one * first[:, columns(step)].astype(F32) + (1.0 - beta_one) * grad
        second_new = (
            beta_two * second[:, columns(step)].astype(F32) + (1.0 - beta_two) * grad * grad
        )
        wide = of(thetas, thetas_last, step)[dp].astype(F32)
        step_size = first_new / (jnp.sqrt(second_new) + adam_epsilon) + decay_rate * wide
        return (wide - inner_rate * step_size).astype(BF16)

    def update_away(step):
        new_theta[step] = update(step)
        share_island(step).start()

    loads[3].wait()
    pack(0)
    pl.semaphore_wait(barrier, greeted)
    send(0)
    for step in range(1, min(AHEAD, steps)):
        pack(step)
        send(step)

    for step in range(steps):
        theta_load(step).start()
    lax.fori_loop(0, blocks, load_saved, 0)
    for load in loads[4:]:
        load.start()
    hidden_acc[...] = jnp.zeros_like(hidden_acc)
    for step in range(steps):
        theta_load(step).wait()
    for step in range(min(AHEAD, steps)):
        share_theta(step).start()
    pltpu.make_async_copy(saved, saved, saved_sem).wait()
    saved_t[...] = saved[...].T
    for load in loads[4:]:
        load.wait()

    def pass_along(step):
        arrived(step, recv_sem).wait()
        pass_on(step).start()

    def advance(step):
        share_theta(step).start()
        pack(step)
        send(step)

    def run(t, carry):
        pass_along(t)

        @pl.when(t + AHEAD < away)
        def _():
            advance(t + AHEAD)

        for step in range(away, steps):

            @pl.when(t + AHEAD_LAST == step)
            def _():
                advance(step)

        @pl.when(t >= 1)
        def _():
            contract(t - 1)

        @pl.when(t >= 2)
        def _():
            update_away(t - 2)

        return carry

    lax.fori_loop(0, away, run, 0)
    for step in range(away + AHEAD_LAST, steps):
        advance(step)

    pass_along(away)
    contract(away - 1)
    if away >= 2:
        update_away(away - 2)
    for step in range(away + 1, steps):
        pass_along(step)
    contract(away)
    update_away(away - 1)
    for step in range(away + 1, steps):
        contract(step)

    for k in range(blocks):
        at = pl.ds(pl.multiple_of(canonical(k) * CAP, CAP), CAP)
        hidden_out[at, :] = (scale * hidden_acc[k * CAP : (k + 1) * CAP, :]).astype(BF16)

    others = jnp.zeros((theta_rows, share), F32)
    for hop in range(1, n_island):
        source = (island + hop) % n_island
        landed = all_theta.at[source]
        pltpu.make_async_copy(landed, landed, island_recv.at[source]).wait()
        others += landed[...].astype(F32)

    for step in range(steps):
        arrived(step, send_sem).wait()
        pass_on(step).wait_send()
        share_theta(step).wait_send()
        share_grad(step).wait_send()
        if step < away:
            share_island(step).wait_send()

    for step in range(away, steps):
        at = slice((step - away) * narrow, (step - away + 1) * narrow)
        mean_delta = anchor[:, at] - (others[:, at] + update(step).astype(F32)) / n_island
        momentum_new = outer_beta * momentum[:, at] + mean_delta
        momentum_out[:, at] = momentum_new
        anchor_out[:, at] = anchor[:, at] - outer_rate * (mean_delta + outer_beta * momentum_new)


def store(anchor, momentum, hidden, anchor_hbm, momentum_hbm, hidden_hbm, sems):
    copies = [
        pltpu.make_async_copy(src, dst, sems.at[k])
        for k, (src, dst) in enumerate(
            [(anchor, anchor_hbm), (momentum, momentum_hbm), (hidden, hidden_hbm)]
        )
    ]
    for copy in copies:
        copy.start()
    for copy in copies:
        copy.wait()


def per_device(
    n_island,
    n_expert,
    theta,
    first_moment,
    second_moment,
    anchor,
    momentum,
    cotangent,
    weights,
    expert_ids,
    expert_counts,
    hidden_saved,
):
    away = n_island - 1
    steps = away + LAST
    theta_rows, features = theta.shape[2:]
    share = features // n_island
    narrow = share // LAST
    slots, units = hidden_saved.shape[3:]
    experts = n_expert // HALVES
    tokens, top = expert_ids.shape
    dma = pltpu.SemaphoreType.DMA

    def both(*shape):
        return (
            pltpu.VMEM((away, *shape, share), BF16),
            pltpu.VMEM((LAST, *shape, narrow), BF16),
        )

    vmem = pl.BlockSpec(memory_space=pltpu.VMEM)
    hbm = pl.BlockSpec(memory_space=pltpu.HBM)
    results = (
        jax.ShapeDtypeStruct((theta_rows, share), F32),
        jax.ShapeDtypeStruct((theta_rows, share), F32),
        jax.ShapeDtypeStruct((slots, units), BF16),
    )
    fresh = pl.pallas_call(
        functools.partial(body, n_island, n_expert),
        out_shape=results,
        in_specs=[hbm] * 10,
        out_specs=(vmem,) * 3,
        scratch_shapes=[
            pltpu.VMEM((top, tokens), jnp.int32),
            pltpu.VMEM((top, tokens), F32),
            pltpu.VMEM((1, experts), jnp.int32),
            pltpu.VMEM((tokens, features), BF16),
            pltpu.VMEM((slots, units), BF16),
            pltpu.VMEM((units, slots), BF16),
            pltpu.VMEM((theta_rows, features), BF16),
            pltpu.VMEM((theta_rows, features), BF16),
            pltpu.VMEM((theta_rows, share), F32),
            pltpu.VMEM((theta_rows, share), F32),
            pltpu.VMEM((3, experts * CAP, tokens), BF16),
            *both(experts, CAP),
            *both(HALVES, slots // HALVES),
            *both(2, theta_rows),
            *both(2, theta_rows),
            *both(theta_rows),
            pltpu.VMEM((away, theta_rows, share), BF16),
            pltpu.VMEM((n_island, theta_rows, share), BF16),
            pltpu.VMEM((slots, units), F32),
            dma((8,)),
            dma,
            dma((steps,)),
            dma((steps,)),
            dma((steps,)),
            dma((steps,)),
            dma((steps,)),
            dma((steps,)),
            dma((steps,)),
            dma((steps,)),
            dma((steps,)),
            dma((steps,)),
            dma((n_island,)),
        ],
        compiler_params=pltpu.CompilerParams(
            collective_id=0, has_side_effects=True, vmem_limit_bytes=VMEM_LIMIT
        ),
        name="diloco_step",
    )(
        *(
            pltpu.with_memory_space_constraint(x, pltpu.HBM)
            for x in (
                expert_ids.T,
                weights.T,
                expert_counts,
                theta.reshape(theta_rows, features),
                first_moment.reshape(theta_rows, features),
                second_moment.reshape(theta_rows, features),
                anchor.reshape(theta_rows, share),
                momentum.reshape(theta_rows, share),
                cotangent,
                hidden_saved.reshape(slots, units),
            )
        )
    )
    anchor_new, momentum_new, d_hidden = pl.pallas_call(
        store,
        out_shape=results,
        in_specs=[vmem] * 3,
        out_specs=(hbm,) * 3,
        scratch_shapes=[dma((3,))],
        name="store",
    )(*(pltpu.with_memory_space_constraint(x, pltpu.VMEM) for x in fresh))
    return (
        anchor_new.reshape(anchor.shape),
        momentum_new.reshape(momentum.shape),
        d_hidden.reshape(hidden_saved.shape),
    )


def solution(mesh):
    return jax.shard_map(
        functools.partial(per_device, mesh.shape["island"], mesh.shape["expert"]),
        mesh=mesh,
        in_specs=(
            P("island", "expert", "dp", None),
            P("island", "expert", "dp", None),
            P("island", "expert", "dp", None),
            P("expert", "dp", "island"),
            P("expert", "dp", "island"),
            P(("island", "dp", "expert"), None),
            P(("island", "dp", "expert"), None),
            P(("island", "dp", "expert"), None),
            P(("island", "dp", "expert"), None),
            P("island", "dp", "expert", None, None),
        ),
        out_specs=(
            P("expert", "dp", "island"),
            P("expert", "dp", "island"),
            P("island", "dp", "expert", None, None),
        ),
        check_vma=False,
    )
```

```python
import functools

import jax
import jax.numpy as jnp
from jax import lax
from jax.experimental import pallas as pl
from jax.experimental.pallas import tpu as pltpu
from jax.sharding import PartitionSpec as P

FF = 768
CAP = 16
CORES = 2
HALVES = 2
GROUPS = 2
LAST = 1
AHEAD = 3
AHEAD_LAST = 3

beta_one = 0.9
beta_two = 0.95
adam_epsilon = 1e-08
inner_rate = 0.1
decay_rate = 0.1
outer_beta = 0.9
outer_rate = 0.7

VMEM_LIMIT = 48 << 20
MESH = pl.DeviceIdType.MESH
F32 = jnp.float32
BF16 = jnp.bfloat16


def dot(a, b, dims):
    return lax.dot_general(a, b, (dims, ((), ())), preferred_element_type=F32)


def body(
    n_island,
    n_expert,
    ids_hbm,
    weights_hbm,
    counts_hbm,
    theta_hbm,
    first_hbm,
    second_hbm,
    anchor_hbm,
    momentum_hbm,
    cot_hbm,
    saved_hbm,
    anchor_out,
    momentum_out,
    hidden_out,
    ids_ref,
    weights_ref,
    counts_ref,
    cot,
    saved,
    saved_t,
    first,
    second,
    anchor,
    momentum,
    picks,
    packed,
    packed_last,
    slots,
    slots_last,
    thetas,
    thetas_last,
    partial,
    partial_last,
    partner_partial,
    partner_partial_last,
    new_theta,
    all_theta,
    hidden_acc,
    load_sem,
    saved_sem,
    theta_sem,
    send_sem,
    recv_sem,
    pass_send,
    pass_recv,
    theta_send,
    theta_recv,
    grad_send,
    grad_recv,
    island_send,
    island_recv,
):
    ring = n_expert // GROUPS
    pairs = ring // HALVES
    half_pairs = pairs // 2
    per_half = ring // HALVES
    experts = GROUPS * pairs
    rows = GROUPS * per_half * CAP
    away = n_island - 1
    steps = away + LAST
    share = cot.shape[1] // n_island
    narrow = share // LAST
    theta_rows = thetas.shape[2]
    tokens = cot.shape[0]
    scale = FF ** (-0.5)

    island = lax.axis_index("island")
    dp = lax.axis_index("dp")
    me = lax.axis_index("expert")
    group = me // ring
    z = me % ring
    pair = z // HALVES
    half = z % HALVES
    partner = group * ring + pair * HALVES + (1 - half)
    other_dp = 1 - dp

    def owner_of(step):
        apart = n_island - 1 - step
        chip = (island // CORES + apart // CORES) % (n_island // CORES)
        return chip * CORES + (island % CORES + apart % CORES) % CORES

    def last(step):
        return isinstance(step, int) and step >= away

    def columns(step):
        if last(step):
            start = island * share + (step - away) * narrow
            return pl.ds(pl.multiple_of(start, narrow), narrow)
        return pl.ds(pl.multiple_of(owner_of(step) * share, share), share)

    def of(wide, cut, step):
        return cut.at[step - away] if last(step) else wide.at[step]

    loads = [
        pltpu.make_async_copy(src, dst, load_sem.at[k])
        for k, (src, dst) in enumerate(
            [
                (ids_hbm, ids_ref),
                (weights_hbm, weights_ref),
                (counts_hbm, counts_ref),
                (cot_hbm, cot),
                (first_hbm, first),
                (second_hbm, second),
                (anchor_hbm, anchor),
                (momentum_hbm, momentum),
            ]
        )
    ]

    barrier = pltpu.get_barrier_semaphore()
    greeted = 0
    for other in range(GROUPS):
        for k in range(per_half):
            if other == 0 and k == 0:
                continue
            source_group = (group + other) % GROUPS
            source_z = (z + (2 * half - 1) * k + ring) % ring
            pl.semaphore_signal(
                barrier,
                inc=1,
                device_id={"expert": source_group * ring + source_z},
                device_id_type=MESH,
            )
            greeted += 1
    pl.semaphore_signal(barrier, inc=1, device_id={"expert": partner}, device_id_type=MESH)
    pl.semaphore_signal(barrier, inc=1, device_id={"dp": other_dp}, device_id_type=MESH)
    greeted += 2
    for k in range(1, n_island):
        pl.semaphore_signal(
            barrier, inc=1, device_id={"island": (island + k) % n_island}, device_id_type=MESH
        )
        greeted += 1

    for load in loads[:4]:
        load.start()

    def theta_load(step):
        return pltpu.make_async_copy(
            theta_hbm.at[:, columns(step)], of(thetas, thetas_last, step).at[dp], theta_sem.at[step]
        )

    def canonical(k):
        which = k // (GROUPS * per_half)
        other = (k // per_half) % GROUPS
        q = k % per_half
        source_z = (pair * HALVES - (per_half - 1) + per_half * which + q + ring) % ring
        return other * ring + source_z

    blocks = HALVES * GROUPS * per_half

    def load_saved(k, carry):
        pltpu.make_async_copy(
            saved_hbm.at[pl.ds(pl.multiple_of(canonical(k) * CAP, CAP), CAP)],
            saved.at[pl.ds(pl.multiple_of(k * CAP, CAP), CAP)],
            saved_sem,
        ).start()
        return carry

    for load in loads[:3]:
        load.wait()
    ids = ids_ref[...]
    weights = weights_ref[...]
    expert_of = lax.broadcasted_iota(jnp.int32, (experts, tokens), 0)
    named = jnp.zeros((experts, tokens), F32)
    weight = jnp.zeros((experts, tokens), F32)
    for k in range(ids.shape[0]):
        hit = ids[k : k + 1, :] == expert_of
        named = jnp.where(hit, 1.0, named)
        weight = jnp.where(hit, weights[k : k + 1, :], weight)
    before = (
        lax.broadcasted_iota(jnp.int32, (tokens, tokens), 0)
        < lax.broadcasted_iota(jnp.int32, (tokens, tokens), 1)
    )
    rank = dot(
        named.astype(BF16), jnp.where(before, 1.0, 0.0).astype(BF16), ((1,), (0,))
    ).astype(jnp.int32)
    diagonal = lax.broadcasted_iota(jnp.int32, (experts, experts), 0) == lax.broadcasted_iota(
        jnp.int32, (experts, experts), 1
    )
    count = jnp.sum(
        jnp.where(diagonal, counts_ref[...].astype(F32), 0.0), axis=1, keepdims=True
    ).astype(jnp.int32)
    rank = jnp.where((named > 0.0) & (rank < count), rank, CAP)
    slot_of = lax.broadcasted_iota(jnp.int32, (experts, CAP, tokens), 1)
    table = jnp.where(rank[:, None, :] == slot_of, weight[:, None, :], 0.0)
    table = table.reshape(experts * CAP, tokens)
    high = table.astype(BF16)
    rest = table - high.astype(F32)
    middle = rest.astype(BF16)
    picks[0] = high
    picks[1] = middle
    picks[2] = (rest - middle.astype(F32)).astype(BF16)

    own_row = (group * per_half + (1 - half) * (per_half - 1)) * CAP
    own_expert = group * pairs + pair

    def pack(step):
        chunk = cot[:, columns(step)]
        rows_out = sum(dot(picks[k], chunk, ((1,), (0,))) for k in range(3))
        to = of(packed, packed_last, step)
        to[...] = rows_out.astype(BF16).reshape(experts, CAP, -1)
        own = of(slots, slots_last, step).at[half, pl.ds(pl.multiple_of(own_row, CAP), CAP)]
        own[...] = to[own_expert]

    def sends(step):
        copies = []
        for d in (half_pairs, *range(half_pairs - 1, 0, -1), *range(half_pairs + 1, pairs), 0):
            for other in range(GROUPS):
                if other == 0 and d == 0:
                    continue
                to_group = (group + other) % GROUPS
                to_pair = (pair + d) % pairs
                if d == 0:
                    to_half = half
                elif d == half_pairs:
                    to_half = 1 - half
                else:
                    to_half = 0 if d < half_pairs else 1
                place = (half - 2 * d + per_half - 1 - per_half * to_half + 3 * ring) % ring
                row = (group * per_half + place) * CAP
                copies.append(
                    pltpu.make_async_remote_copy(
                        of(packed, packed_last, step).at[to_group * pairs + to_pair],
                        of(slots, slots_last, step).at[
                            to_half, pl.ds(pl.multiple_of(row, CAP), CAP)
                        ],
                        send_sem.at[step],
                        recv_sem.at[step, other],
                        device_id={"expert": to_group * ring + to_pair * HALVES + to_half},
                        device_id_type=MESH,
                    )
                )
        return copies

    def send(step):
        for copy in sends(step):
            copy.start()

    def arrived(step, sem):
        some = of(slots, slots_last, step).at[0, pl.ds(0, rows - CAP)]
        return pltpu.make_async_copy(some, some, sem.at[step])

    def arrived_from(step, other):
        size = rows // GROUPS - (CAP if other == 0 else 0)
        some = of(slots, slots_last, step).at[0, pl.ds(0, size)]
        return pltpu.make_async_copy(some, some, recv_sem.at[step, other])

    def pass_on(step, other):
        size = rows // GROUPS
        at = pl.ds(pl.multiple_of((group + other) % GROUPS * size, size), size)
        return pltpu.make_async_remote_copy(
            of(slots, slots_last, step).at[half, at],
            of(slots, slots_last, step).at[half, at],
            pass_send.at[step, other],
            pass_recv.at[step, other],
            device_id={"expert": partner},
            device_id_type=MESH,
        )

    def share_theta(step):
        return pltpu.make_async_remote_copy(
            of(thetas, thetas_last, step).at[dp],
            of(thetas, thetas_last, step).at[dp],
            theta_send.at[step],
            theta_recv.at[step],
            device_id={"dp": other_dp},
            device_id_type=MESH,
        )

    def share_grad(step):
        return pltpu.make_async_remote_copy(
            of(partial, partial_last, step).at[other_dp],
            of(partner_partial, partner_partial_last, step),
            grad_send.at[step],
            grad_recv.at[step],
            device_id={"dp": other_dp},
            device_id_type=MESH,
        )

    def share_island(step):
        owner = owner_of(step)
        return pltpu.make_async_remote_copy(
            new_theta.at[step],
            all_theta.at[island],
            island_send.at[step],
            island_recv.at[island],
            device_id={"island": owner},
            device_id_type=MESH,
        )

    def contract(step):
        for other in range(GROUPS):
            pass_on(step, other).wait_recv()
        chunk = of(slots, slots_last, step)[...].reshape(HALVES * rows, -1)
        to = of(partial, partial_last, step)

        def product(part):
            at = pl.ds(pl.multiple_of(part * theta_rows, theta_rows), theta_rows)
            return (scale * dot(saved_t[at, :], chunk, ((1,), (0,)))).astype(BF16)

        to[other_dp] = product(other_dp)
        share_grad(step).start()
        to[dp] = product(dp)
        share_theta(step).wait_recv()
        full = of(thetas, thetas_last, step)[...].reshape(2 * theta_rows, -1)
        hidden_acc[...] += dot(chunk, full, ((1,), (1,)))

    def update(step):
        share_grad(step).wait_recv()
        mine = of(partial, partial_last, step)[dp].astype(F32)
        grad = mine + of(partner_partial, partner_partial_last, step)[...].astype(F32)
        first_new = beta_one * first[:, columns(step)].astype(F32) + (1.0 - beta_one) * grad
        second_new = (
            beta_two * second[:, columns(step)].astype(F32) + (1.0 - beta_two) * grad * grad
        )
        wide = of(thetas, thetas_last, step)[dp].astype(F32)
        step_size = first_new / (jnp.sqrt(second_new) + adam_epsilon) + decay_rate * wide
        return (wide - inner_rate * step_size).astype(BF16)

    def update_away(step):
        new_theta[step] = update(step)
        share_island(step).start()

    loads[3].wait()
    pack(0)
    pl.semaphore_wait(barrier, greeted)
    send(0)
    for step in range(1, min(AHEAD, steps)):
        pack(step)
        send(step)

    for step in range(steps):
        theta_load(step).start()
    lax.fori_loop(0, blocks, load_saved, 0)
    for load in loads[4:]:
        load.start()
    hidden_acc[...] = jnp.zeros_like(hidden_acc)
    for step in range(steps):
        theta_load(step).wait()
    for step in range(min(AHEAD, steps)):
        share_theta(step).start()
    pltpu.make_async_copy(saved, saved, saved_sem).wait()
    saved_t[...] = saved[...].T
    for load in loads[4:]:
        load.wait()

    def pass_along(step):
        for other in range(GROUPS):
            arrived_from(step, other).wait()
            pass_on(step, other).start()

    def advance(step):
        share_theta(step).start()
        pack(step)
        send(step)

    def run(t, carry):
        pass_along(t)

        @pl.when(t + AHEAD < away)
        def _():
            advance(t + AHEAD)

        for step in range(away, steps):

            @pl.when(t + AHEAD_LAST == step)
            def _():
                advance(step)

        @pl.when(t >= 1)
        def _():
            contract(t - 1)

        @pl.when(t >= 2)
        def _():
            update_away(t - 2)

        return carry

    lax.fori_loop(0, away, run, 0)
    for step in range(away + AHEAD_LAST, steps):
        advance(step)

    pass_along(away)
    contract(away - 1)
    if away >= 2:
        update_away(away - 2)
    for step in range(away + 1, steps):
        pass_along(step)
    contract(away)
    update_away(away - 1)
    for step in range(away + 1, steps):
        contract(step)

    for k in range(blocks):
        at = pl.ds(pl.multiple_of(canonical(k) * CAP, CAP), CAP)
        hidden_out[at, :] = (scale * hidden_acc[k * CAP : (k + 1) * CAP, :]).astype(BF16)

    others = jnp.zeros((theta_rows, share), F32)
    for hop in range(1, n_island):
        source = (island + hop) % n_island
        landed = all_theta.at[source]
        pltpu.make_async_copy(landed, landed, island_recv.at[source]).wait()
        others += landed[...].astype(F32)

    for step in range(steps):
        arrived(step, send_sem).wait()
        for other in range(GROUPS):
            pass_on(step, other).wait_send()
        share_theta(step).wait_send()
        share_grad(step).wait_send()
        if step < away:
            share_island(step).wait_send()

    for step in range(away, steps):
        at = slice((step - away) * narrow, (step - away + 1) * narrow)
        mean_delta = anchor[:, at] - (others[:, at] + update(step).astype(F32)) / n_island
        momentum_new = outer_beta * momentum[:, at] + mean_delta
        momentum_out[:, at] = momentum_new
        anchor_out[:, at] = anchor[:, at] - outer_rate * (mean_delta + outer_beta * momentum_new)


def store(anchor, momentum, hidden, anchor_hbm, momentum_hbm, hidden_hbm, sems):
    copies = [
        pltpu.make_async_copy(src, dst, sems.at[k])
        for k, (src, dst) in enumerate(
            [(anchor, anchor_hbm), (momentum, momentum_hbm), (hidden, hidden_hbm)]
        )
    ]
    for copy in copies:
        copy.start()
    for copy in copies:
        copy.wait()


def per_device(
    n_island,
    n_expert,
    theta,
    first_moment,
    second_moment,
    anchor,
    momentum,
    cotangent,
    weights,
    expert_ids,
    expert_counts,
    hidden_saved,
):
    away = n_island - 1
    steps = away + LAST
    theta_rows, features = theta.shape[2:]
    share = features // n_island
    narrow = share // LAST
    slots, units = hidden_saved.shape[3:]
    experts = n_expert // HALVES
    tokens, top = expert_ids.shape
    dma = pltpu.SemaphoreType.DMA

    def both(*shape):
        return (
            pltpu.VMEM((away, *shape, share), BF16),
            pltpu.VMEM((LAST, *shape, narrow), BF16),
        )

    vmem = pl.BlockSpec(memory_space=pltpu.VMEM)
    hbm = pl.BlockSpec(memory_space=pltpu.HBM)
    results = (
        jax.ShapeDtypeStruct((theta_rows, share), F32),
        jax.ShapeDtypeStruct((theta_rows, share), F32),
        jax.ShapeDtypeStruct((slots, units), BF16),
    )
    fresh = pl.pallas_call(
        functools.partial(body, n_island, n_expert),
        out_shape=results,
        in_specs=[hbm] * 10,
        out_specs=(vmem,) * 3,
        scratch_shapes=[
            pltpu.VMEM((top, tokens), jnp.int32),
            pltpu.VMEM((top, tokens), F32),
            pltpu.VMEM((1, experts), jnp.int32),
            pltpu.VMEM((tokens, features), BF16),
            pltpu.VMEM((slots, units), BF16),
            pltpu.VMEM((units, slots), BF16),
            pltpu.VMEM((theta_rows, features), BF16),
            pltpu.VMEM((theta_rows, features), BF16),
            pltpu.VMEM((theta_rows, share), F32),
            pltpu.VMEM((theta_rows, share), F32),
            pltpu.VMEM((3, experts * CAP, tokens), BF16),
            *both(experts, CAP),
            *both(HALVES, slots // HALVES),
            *both(2, theta_rows),
            *both(2, theta_rows),
            *both(theta_rows),
            pltpu.VMEM((away, theta_rows, share), BF16),
            pltpu.VMEM((n_island, theta_rows, share), BF16),
            pltpu.VMEM((slots, units), F32),
            dma((8,)),
            dma,
            dma((steps,)),
            dma((steps,)),
            dma((steps, GROUPS)),
            dma((steps, GROUPS)),
            dma((steps, GROUPS)),
            dma((steps,)),
            dma((steps,)),
            dma((steps,)),
            dma((steps,)),
            dma((steps,)),
            dma((n_island,)),
        ],
        compiler_params=pltpu.CompilerParams(
            collective_id=0, has_side_effects=True, vmem_limit_bytes=VMEM_LIMIT
        ),
        name="diloco_step",
    )(
        *(
            pltpu.with_memory_space_constraint(x, pltpu.HBM)
            for x in (
                expert_ids.T,
                weights.T,
                expert_counts,
                theta.reshape(theta_rows, features),
                first_moment.reshape(theta_rows, features),
                second_moment.reshape(theta_rows, features),
                anchor.reshape(theta_rows, share),
                momentum.reshape(theta_rows, share),
                cotangent,
                hidden_saved.reshape(slots, units),
            )
        )
    )
    anchor_new, momentum_new, d_hidden = pl.pallas_call(
        store,
        out_shape=results,
        in_specs=[vmem] * 3,
        out_specs=(hbm,) * 3,
        scratch_shapes=[dma((3,))],
        name="store",
    )(*(pltpu.with_memory_space_constraint(x, pltpu.VMEM) for x in fresh))
    return (
        anchor_new.reshape(anchor.shape),
        momentum_new.reshape(momentum.shape),
        d_hidden.reshape(hidden_saved.shape),
    )


def solution(mesh):
    return jax.shard_map(
        functools.partial(per_device, mesh.shape["island"], mesh.shape["expert"]),
        mesh=mesh,
        in_specs=(
            P("island", "expert", "dp", None),
            P("island", "expert", "dp", None),
            P("island", "expert", "dp", None),
            P("expert", "dp", "island"),
            P("expert", "dp", "island"),
            P(("island", "dp", "expert"), None),
            P(("island", "dp", "expert"), None),
            P(("island", "dp", "expert"), None),
            P(("island", "dp", "expert"), None),
            P("island", "dp", "expert", None, None),
        ),
        out_specs=(
            P("expert", "dp", "island"),
            P("expert", "dp", "island"),
            P("island", "dp", "expert", None, None),
        ),
        check_vma=False,
    )
```
